256 devices in a mesh: expert: 64 (over z, y, core), replica: 4 (over x).
Axes of the slice: x: 4, y: 4, z: 8, core: 2. Of those that a mesh axis runs over, the one named last changes fastest.
Arguments:
- hidden_first: bfloat16 [2048, 4096], P(('expert', 'replica')), may hold values from -40 to 40
- hidden_second: bfloat16 [2048, 4096], P(('expert', 'replica')), may hold values from -40 to 40
- routes_first: int32 [2048, 8], P(('expert', 'replica')), may hold values from 0 to 63, all different within a row; in each aligned block of 8 rows (0 to 7, 8 to 15, ...) at most 2 rows name the same one
- routes_second: int32 [2048, 8], P(('expert', 'replica')), may hold values from 0 to 63, all different within a row; in each aligned block of 8 rows (0 to 7, 8 to 15, ...) at most 2 rows name the same one
- mixing_first: float32 [2048, 8], P(('expert', 'replica')), may hold values from 0.05 to 0.5
- mixing_second: float32 [2048, 8], P(('expert', 'replica')), may hold values from 0.05 to 0.5
- norm_gain: float32 [4096], replicated, may hold values from 0.1 to 1.9
- expert_owner: int32 [64], replicated, may hold values from 0 to 63, each once
- swap_flags: int32 [64], replicated, may hold values from 0 to 1, as said below
- gate_up_values: bfloat16 [64, 2, 4096, 1024], P('expert', None, None, 'replica'), may hold values from -0.09375 to 0.09375
- gate_up_scales: bfloat16 [64, 2, 32, 8], P('expert', None, None, 'replica'), may hold values from 0.5 to 2
- down_values: bfloat16 [64, 1024, 4096], P('expert', 'replica'), may hold values from -0.1875 to 0.1875
- down_scales: bfloat16 [64, 8, 32], P('expert', 'replica'), may hold values from 0.5 to 2
Outputs:
- output_first: bfloat16 [2048, 4096], P(('expert', 'replica'))
- output_second: bfloat16 [2048, 4096], P(('expert', 'replica'))
- gate_up_moved: bfloat16 [64, 2, 4096, 1024], P('expert', None, None, 'replica')
- gate_up_scales_moved: bfloat16 [64, 2, 32, 8], P('expert', None, None, 'replica')
- down_moved: bfloat16 [64, 1024, 4096], P('expert', 'replica')
- down_scales_moved: bfloat16 [64, 8, 32], P('expert', 'replica')
The draws below stay inside these ranges and needn't reach their ends.
Inputs may be any that keep to these rules, and one draw needn't show every extreme that they name: swap_flags[d] equals swap_flags[(d + 32) mod 64].
All inputs are finite; a program needn't handle non-finite values.
Results may differ from the reference program's by a relative error of at most 0.012.
Values may be sent and summed in bfloat16 or wider, within the bound.
No kernel may reach another device: no remote copies, remote signals or barrier semaphores. Data moves between devices by JAX's collectives and lax.ppermute only.
A program may use at most 128 MiB of HBM per device.

```python
import math
import jax
import jax.numpy as jnp
import numpy as np
from jax import lax

D = 4096
FFW = 1024
TOPK = 8
BLOCK = 128
TOK_DEV = 8
EXPERTS = 64
CAP = 2
TOKENS = 2048
N_EXPERT = 64
N_REPLICA = 4


def spread_field(key):
    base_key, row_key, col_key = jax.random.split(key, 3)
    values = jnp.clip(jax.random.normal(base_key, (TOKENS, D), jnp.float32), -4.0, 4.0)
    row_scale = jnp.exp(jax.random.uniform(row_key, (TOKENS, 1), jnp.float32, -1.15, 1.15))
    col_scale = jnp.exp(jax.random.uniform(col_key, (1, D), jnp.float32, -1.15, 1.15))
    return values * row_scale * col_scale


def draw_hidden_first(key, part):
    return spread_field(jax.random.fold_in(key, 11)).astype(jnp.bfloat16)


def draw_hidden_second(key, part):
    return spread_field(jax.random.fold_in(key, 23)).astype(jnp.bfloat16)


def draw_swap_flags(key, part):
    halfway = EXPERTS // 2
    leading = jax.random.randint(jax.random.fold_in(key, 37), (halfway,), 0, 2).astype(jnp.int32)
    leading = leading.at[0].set(1).at[1].set(0)
    return jnp.concatenate([leading, leading])


def shard_levels(rng, extent, pieces, smallest, top_value):
    gain, own = 1.0, jax.random.fold_in(rng, 6)
    for axis_at, parts in pieces:
        heights = jnp.exp(jax.random.uniform(jax.random.fold_in(own, axis_at), (parts,), jnp.float32, smallest / len(pieces), top_value / len(pieces)))
        gain = gain * jnp.repeat(heights, extent[axis_at] // parts).reshape([-1 if axis == axis_at else 1 for axis in range(len(extent))])
    return gain


def shared_out(rng, own, number, rows, count, top, most, lean):
    order = jax.random.permutation(rng, count)
    crowded, common = load_shares(count, rows * top, most, lean, True), load_shares(count, rows * top, most, lean, False)
    places = jnp.arange(count)

    def named(lengths, turn):
        used = int((lengths > 0).sum())
        fixed = max(1, used // 4)
        passed = fixed + (places - fixed + turn * (used - fixed)) % max(1, count - fixed)
        return jnp.zeros((count,), jnp.int32).at[order[jnp.where(places < fixed, places, passed)]].set(jnp.asarray(lengths, jnp.int32))

    lengths = jnp.where(number % 4 == 0, named(crowded, number // 4), named(common, number - number // 4 - 1))
    mixed = jax.random.permutation(jax.random.fold_in(own, 3), count)
    source_of, taker = mixed[0:count // 2 * 2:2], mixed[1:count // 2 * 2:2]
    margin = jnp.minimum(lengths[source_of] - 1, most - lengths[taker]) // 2
    margin = jnp.where((source_of == order[0]) | (taker == order[0]) | (lengths[taker] == 0), 0, jnp.maximum(margin, 0))
    passed = jax.random.randint(jax.random.fold_in(own, 4), (count // 2,), 0, 1 << 20) % (margin + 1)
    lengths = lengths.at[source_of].add(-passed).at[taker].add(passed)
    items = jnp.searchsorted(jnp.cumsum(lengths), jnp.arange(rows * top), side="right").astype(jnp.int32)
    table = items.reshape(top, rows).T
    table = table[jax.random.permutation(jax.random.fold_in(own, 1), rows)]
    turn = jax.random.randint(jax.random.fold_in(own, 2), (rows, 1), 0, top)
    return jnp.take_along_axis(table, (jnp.arange(top)[None, :] + turn) % top, axis=1)


def load_shares(number_of, total, most, slope, full):
    weights = [(1 << 20) // math.isqrt(standing ** slope) + 1 for standing in range(1, number_of + 1)]
    largest = most if full else min(most, max(-(-total // number_of), total * weights[0] // sum(weights)))
    least = 1 if total - largest >= number_of - 1 else 0
    counts, spare = [largest] + [least] * (number_of - 1), total - largest - least * (number_of - 1)
    while spare > 0:
        movable = [i for i in range(1, number_of) if counts[i] < largest] or [i for i in range(1, number_of) if counts[i] < most]
        pool, budget = sum([weights[i] for i in movable]), spare
        for i in movable:
            addition = min(most - counts[i], max(1, budget * weights[i] // pool), spare)
            counts[i] = counts[i] + addition
            spare = spare - addition
    return np.array(counts)


def normal_values(rng, extent, deviation, bound, cuts=(), kind=jnp.bfloat16):
    entries = deviation * jax.random.normal(rng, extent, jnp.float32)
    if cuts:
        entries = entries * shard_levels(rng, extent, cuts, -0.22, 0.18)
    return jnp.clip(entries, -bound, bound).astype(kind)


def setup_inputs(seed: int = 0) -> dict:
    splits = jax.random.split(jax.random.key(seed), 14)
    hidden_first = draw_hidden_first(jax.random.fold_in(splits[13], 71), 0)
    hidden_second = draw_hidden_second(jax.random.fold_in(splits[13], 71), 0)
    routes_first_keys = jax.random.split(jax.random.fold_in(splits[2], 1), TOKENS // TOK_DEV)
    routes_first_turns = jax.random.permutation(jax.random.fold_in(splits[2], 3), TOKENS // TOK_DEV)
    routes_first = jax.vmap(lambda own, number: shared_out(jax.random.fold_in(splits[2], 2), own, number, TOK_DEV, EXPERTS, TOPK, CAP, 2))(routes_first_keys, routes_first_turns).reshape((TOKENS, TOPK))
    routes_second_keys = jax.random.split(jax.random.fold_in(splits[3], 1), TOKENS // TOK_DEV)
    routes_second_turns = jax.random.permutation(jax.random.fold_in(splits[3], 3), TOKENS // TOK_DEV)
    routes_second = jax.vmap(lambda own, number: shared_out(jax.random.fold_in(splits[3], 2), own, number, TOK_DEV, EXPERTS, TOPK, CAP, 2))(routes_second_keys, routes_second_turns).reshape((TOKENS, TOPK))
    mixing_first = jnp.clip(jnp.exp(math.log(0.5) - 2.3025851 * jax.random.uniform(splits[4], (TOKENS, TOPK), jnp.float32) ** shard_levels(splits[4], (TOKENS, TOPK), ((0, 256),), -0.2, 0.2)), 0.05, 0.5)
    mixing_second = jnp.clip(jnp.exp(math.log(0.5) - 2.3025851 * jax.random.uniform(splits[5], (TOKENS, TOPK), jnp.float32) ** shard_levels(splits[5], (TOKENS, TOPK), ((0, 256),), -0.2, 0.2)), 0.05, 0.5)
    norm_gain = jnp.clip(1.0 + 0.18 * jax.random.normal(splits[6], (D,), jnp.float32), 0.1, 1.9)
    expert_owner = jax.random.permutation(splits[7], EXPERTS).astype(jnp.int32)
    swap_flags = draw_swap_flags(jax.random.fold_in(splits[13], 71), 0)
    gate_up_values = normal_values(splits[9], (EXPERTS, 2, D, FFW), D ** -0.5, 0.09375, ((0, 64), (3, 4)))
    gate_up_scales = jnp.clip(jnp.exp(math.log(2.0) - 1.3862944 * jax.random.uniform(splits[10], (EXPERTS, 2, D // BLOCK, FFW // BLOCK), jnp.float32) ** shard_levels(splits[10], (EXPERTS, 2, D // BLOCK, FFW // BLOCK), ((0, 64), (3, 4)), -0.2, 0.2)), 0.5, 2.0).astype(jnp.bfloat16)
    down_values = normal_values(splits[11], (EXPERTS, FFW, D), FFW ** -0.5, 0.1875, ((0, 64), (1, 4)))
    down_scales = jnp.clip(jnp.exp(math.log(2.0) - 1.3862944 * jax.random.uniform(splits[12], (EXPERTS, FFW // BLOCK, D // BLOCK), jnp.float32) ** shard_levels(splits[12], (EXPERTS, FFW // BLOCK, D // BLOCK), ((0, 64), (1, 4)), -0.2, 0.2)), 0.5, 2.0).astype(jnp.bfloat16)
    return dict(hidden_first=hidden_first, hidden_second=hidden_second, routes_first=routes_first, routes_second=routes_second, mixing_first=mixing_first, mixing_second=mixing_second, norm_gain=norm_gain, expert_owner=expert_owner, swap_flags=swap_flags, gate_up_values=gate_up_values, gate_up_scales=gate_up_scales, down_values=down_values, down_scales=down_scales)


def dequantize(values, scales):
    height, breadth = (values.shape[-2], values.shape[-1])
    block_rows, block_cols = (scales.shape[-2], scales.shape[-1])
    leading = values.shape[:-2]
    blocked = values.astype(jnp.float32).reshape(leading + (block_rows, height // block_rows, block_cols, breadth // block_cols))
    scaled = blocked * scales.astype(jnp.float32)[..., :, None, :, None]
    return scaled.reshape(values.shape).astype(jnp.bfloat16)

def rms_normed(hidden, norm_gain):
    widened = hidden.astype(jnp.float32)
    inverse_rms = lax.rsqrt(lax.optimization_barrier(jnp.mean(widened * widened, axis=-1, keepdims=True)) + 1e-06)
    return (widened * inverse_rms * norm_gain).astype(jnp.bfloat16)

def rounded(partial_sum):
    return lax.optimization_barrier(partial_sum.astype(jnp.bfloat16)).astype(jnp.float32)

def expert_output(token_rows, gate_up, down_proj):
    gate_act = jnp.dot(token_rows, gate_up[0], preferred_element_type=jnp.float32)
    up_act = jnp.dot(token_rows, gate_up[1], preferred_element_type=jnp.float32)
    inner_act = (jax.nn.silu(gate_act) * up_act).astype(jnp.bfloat16)
    share_width = down_proj.shape[0] // N_REPLICA
    running = jnp.zeros((token_rows.shape[0], down_proj.shape[1]), jnp.float32)
    for block_index in range(N_REPLICA):
        lower_edge = block_index * share_width
        partial_piece = jnp.dot(inner_act[:, lower_edge:lower_edge + share_width], down_proj[lower_edge:lower_edge + share_width], preferred_element_type=jnp.float32)
        running = running + rounded(partial_piece)
    return running.astype(jnp.bfloat16)

def layer_step(hidden, routes, mixing, norm_gain, weights_of):
    normed = rms_normed(hidden, norm_gain)
    pick_experts = routes.reshape(-1).astype(jnp.int32)
    pick_tokens = (jnp.arange(pick_experts.shape[0], dtype=jnp.int32) // TOPK).astype(jnp.int32)
    pick_weights = mixing.reshape(-1)
    row_limit = N_EXPERT * N_REPLICA * CAP

    def visit_expert(running, expert_id):
        matches = pick_experts == expert_id
        found_rows = jnp.nonzero(matches, size=row_limit, fill_value=0)[0].astype(jnp.int32)
        filled = (jnp.arange(row_limit, dtype=jnp.int32) < jnp.sum(matches.astype(jnp.int32))).astype(pick_weights.dtype)
        token_ids = pick_tokens[found_rows]
        gate_up, down_proj = weights_of(expert_id)
        result = expert_output(normed[token_ids], gate_up, down_proj).astype(pick_weights.dtype)
        shares = pick_weights[found_rows] * filled
        return (running.at[token_ids].add(result * shares[:, None]), None)
    start_sum = jnp.zeros(hidden.shape, pick_weights.dtype)
    running, _unused = lax.scan(visit_expert, start_sum, jnp.arange(EXPERTS, dtype=jnp.int32))
    return running.astype(jnp.bfloat16)

def reference(hidden_first, hidden_second, routes_first, routes_second, mixing_first, mixing_second, norm_gain, expert_owner, swap_flags, gate_up_values, gate_up_scales, down_values, down_scales):
    slot_ids = jnp.arange(EXPERTS, dtype=jnp.int32)
    source = jnp.where(swap_flags == 1, (slot_ids + EXPERTS // 2) % EXPERTS, slot_ids).astype(jnp.int32)
    moved_arrays = tuple((source_array[source] for source_array in (gate_up_values, gate_up_scales, down_values, down_scales)))

    def weights_of(expert_id):
        home_slot = expert_owner[expert_id]
        return (dequantize(gate_up_values[home_slot], gate_up_scales[home_slot]), dequantize(down_values[home_slot], down_scales[home_slot]))
    output_first = layer_step(hidden_first, routes_first, mixing_first, norm_gain, weights_of)
    output_second = layer_step(hidden_second, routes_second, mixing_second, norm_gain, weights_of)
    return (output_first, output_second, moved_arrays[0], moved_arrays[1], moved_arrays[2], moved_arrays[3])
```

```python
import jax
import jax.numpy as jnp
from jax import lax
from jax.experimental import pallas as pl
from jax.experimental.pallas import tpu as pltpu
from jax.sharding import PartitionSpec as P


BF16 = jnp.bfloat16
F32 = jnp.float32
I32 = jnp.int32
TOK = 8
CAP = 2
LANES = 128
PLANE = 8
VMEM = pltpu.VMEM
SMEM = pltpu.SMEM


def iota(shape, dim):
    return lax.broadcasted_iota(I32, shape, dim)


def vspec():
    return pl.BlockSpec(memory_space=VMEM)


def sspec():
    return pl.BlockSpec(memory_space=SMEM)


def gate_up_dequant(values, scale_rows):
    _, features, width = values.shape
    rows = features // 4
    blocks = rows // LANES

    def kernel(v_ref, s_ref, o_ref):
        wide = v_ref[0].astype(F32).reshape(blocks, LANES, width)
        o_ref[0] = (wide * s_ref[0][:, None, :]).reshape(rows, width).astype(BF16)

    return pl.pallas_call(
        kernel,
        grid=(2, 4),
        in_specs=[
            pl.BlockSpec((1, rows, width), lambda g, i: (g, i, 0)),
            pl.BlockSpec((1, blocks, width), lambda g, i: (g, i, 0)),
        ],
        out_specs=pl.BlockSpec((1, rows, width), lambda g, i: (g, i, 0)),
        out_shape=jax.ShapeDtypeStruct(values.shape, BF16),
        name="gate_up_dequant",
    )(values, scale_rows)


def down_dequant(values, scale_rows, order):
    height, features = values.shape
    copies = order.shape[0]
    width = features // copies
    blocks = scale_rows.shape[0]

    def kernel(order_ref, v_ref, s_ref, o_ref):
        wide = v_ref[...].astype(F32).reshape(blocks, height // blocks, width)
        o_ref[0] = (wide * s_ref[...][:, None, :]).reshape(height, width).astype(BF16)

    return pl.pallas_call(
        kernel,
        grid_spec=pltpu.PrefetchScalarGridSpec(
            num_scalar_prefetch=1,
            grid=(copies,),
            in_specs=[
                pl.BlockSpec((height, width), lambda k, o: (0, o[k])),
                pl.BlockSpec((blocks, width), lambda k, o: (0, o[k])),
            ],
            out_specs=pl.BlockSpec((1, height, width), lambda k, o: (k, 0, 0)),
        ),
        out_shape=jax.ShapeDtypeStruct((copies, height, width), BF16),
        name="down_dequant",
    )(order, values, scale_rows)


def norm_and_pack(hidden, ids, gain):
    rows, features = hidden[0].shape

    def kernel(h0, h1, i0, i1, g_ref, o_ref):
        for at, h_ref, i_ref in ((0, h0, i0), (rows, h1, i1)):
            wide = h_ref[...].astype(F32)
            inverse = lax.rsqrt(jnp.mean(wide * wide, axis=-1, keepdims=True) + 1e-06)
            o_ref[at : at + rows, :features] = (wide * inverse * g_ref[...]).astype(BF16)
            o_ref[at : at + rows, features:] = i_ref[...]

    return pl.pallas_call(
        kernel,
        in_specs=[vspec()] * 5,
        out_specs=vspec(),
        out_shape=jax.ShapeDtypeStruct((2 * rows, features + LANES), BF16),
        name="norm_and_pack",
    )(hidden[0], hidden[1], ids[0], ids[1], gain)


def select_rows(gathered, my_expert):
    both, packed = gathered.shape
    features = packed - LANES
    rows = both // 2
    kept = rows // TOK * CAP

    def kernel(e_ref, g_ref, *o_refs):
        mine = e_ref[0].astype(F32)
        r, q = iota((rows, rows), 0), iota((rows, rows), 1)
        before = jnp.where(((r >> 3) == (q >> 3)) & (q < r), 1.0, 0.0).astype(BF16)
        row, col = iota((rows, kept), 0), iota((rows, kept), 1)

        def of_step(step, start, size):
            part = g_ref[:, start : start + size].reshape(rows // TOK, 2, TOK, size)
            return part[:, step].reshape(rows, size)

        for step, o_ref in enumerate(o_refs):
            ids = of_step(step, features, LANES).astype(F32)
            hit = jnp.max(jnp.where(ids == mine, 1.0, 0.0), axis=1, keepdims=True)
            hits = jnp.broadcast_to(hit, (rows, kept))
            rank = jnp.dot(before, hits.astype(BF16), preferred_element_type=F32)
            chosen = ((row >> 3) == (col >> 1)) & (rank == (col & 1).astype(F32)) & (hits > 0.5)
            picking = jnp.where(chosen, 1.0, 0.0).astype(BF16)
            for at in range(0, features, 1024):
                o_ref[:, at : at + 1024] = lax.dot_general(
                    picking,
                    of_step(step, at, 1024),
                    (((0,), (0,)), ((), ())),
                    preferred_element_type=F32,
                ).astype(BF16)

    shape = jax.ShapeDtypeStruct((kept, features), BF16)
    return pl.pallas_call(
        kernel,
        in_specs=[sspec(), vspec()],
        out_specs=[vspec()] * 2,
        out_shape=[shape] * 2,
        name="select_rows",
    )(my_expert, gathered)


def gate_up(pieces, weights, columns):
    copies = len(pieces)
    rows, features = pieces[0].shape
    width = weights.shape[2]

    def kernel(c_ref, *refs):
        x_refs, w_ref, o_ref, x_all = refs[:copies], refs[copies], refs[copies + 1], refs[copies + 2]
        for k in range(copies):
            start = pl.multiple_of(c_ref[k] * rows, rows)
            x_all[pl.ds(start, rows), :] = x_refs[k][...]
        gate = jnp.dot(x_all[...], w_ref[0], preferred_element_type=F32)
        up = jnp.dot(x_all[...], w_ref[1], preferred_element_type=F32)
        o_ref[...] = (gate / (1.0 + jnp.exp(-gate)) * up).astype(BF16)

    return pl.pallas_call(
        kernel,
        in_specs=[sspec()] + [vspec()] * (copies + 1),
        out_specs=vspec(),
        out_shape=jax.ShapeDtypeStruct((copies * rows, width), BF16),
        scratch_shapes=[pltpu.VMEM((copies * rows, features), BF16)],
        name="gate_up",
    )(columns, *pieces, weights)


def down(inner, weights):
    copies = len(inner)
    rows, _ = inner[0].shape
    kept = rows // copies
    width = weights[0].shape[1]

    def kernel(*refs):
        i_refs, w_refs, o_ref = refs[:copies], refs[copies : 2 * copies], refs[2 * copies]
        r, q = iota((rows, rows), 0), iota((rows, rows), 1)
        source = ((r >> 1) & 3) * kept + ((r >> 3) << 1) + (r & 1)
        order = jnp.where(q == source, 1.0, 0.0).astype(BF16)
        total = jnp.zeros((rows, width), F32)
        for i_ref, w_ref in zip(i_refs, w_refs):
            placed = jnp.dot(order, i_ref[...], preferred_element_type=F32).astype(BF16)
            total = total + jnp.dot(placed, w_ref[...], preferred_element_type=F32)
        o_ref[...] = total.astype(BF16)

    return pl.pallas_call(
        kernel,
        in_specs=[vspec()] * (2 * copies),
        out_specs=vspec(),
        out_shape=jax.ShapeDtypeStruct((rows, width), BF16),
        name="down",
    )(*inner, *weights)


def mixing_tables(packed, plane_experts):
    tokens, top = packed.shape[0], packed.shape[1] // 4
    places = plane_experts.shape[1]

    def kernel(p_ref, e_ref, *outs):
        at = e_ref[...].astype(F32)
        r, q = iota((tokens, tokens), 0), iota((tokens, tokens), 1)
        before = jnp.where(((r >> 3) == (q >> 3)) & (q < r), 1.0, 0.0).astype(BF16)
        row, col = iota((tokens, places), 0), iota((tokens, places), 1)
        for step in range(2):
            hit = jnp.zeros((tokens, places), F32)
            weight = jnp.zeros((tokens, places), F32)
            for k in range(top):
                lane = step * 2 * top + k
                same = p_ref[:, lane : lane + 1] == at
                hit = hit + jnp.where(same, 1.0, 0.0)
                weight = weight + jnp.where(same, p_ref[:, lane + top : lane + top + 1], 0.0)
            rank = jnp.dot(before, hit.astype(BF16), preferred_element_type=F32)
            here = (((row >> 3) & 3) == ((col >> 1) & 3)) & (rank == (col & 1).astype(F32))
            kept = jnp.where(here, weight, 0.0)
            high = kept.astype(BF16)
            outs[2 * step][...] = high
            outs[2 * step + 1][...] = (kept - high.astype(F32)).astype(BF16)

    shape = jax.ShapeDtypeStruct((tokens, places), BF16)
    return pl.pallas_call(
        kernel,
        in_specs=[vspec(), vspec()],
        out_specs=[vspec()] * 4,
        out_shape=[shape] * 4,
        name="mixing_tables",
    )(packed, plane_experts)


def combine(returned, tables, copies):
    members, levels, rows, width = returned[0].shape

    def kernel(r0, r1, h0, l0, h1, l1, o_ref):
        for step, (r_ref, h_ref, l_ref) in enumerate(((r0, h0, l0), (r1, h1, l1))):
            for level in range(levels):
                found = r_ref[:, level].reshape(members * rows, width)
                at = slice(level * copies * TOK, (level + 1) * copies * TOK)
                total = jnp.dot(h_ref[at, :], found, preferred_element_type=F32) + jnp.dot(
                    l_ref[at, :], found, preferred_element_type=F32
                )
                o_ref[level, :, step] = total.astype(BF16).reshape(copies, TOK, width)

    return pl.pallas_call(
        kernel,
        in_specs=[vspec()] * 6,
        out_specs=vspec(),
        out_shape=jax.ShapeDtypeStruct((levels, copies, 2, TOK, width), BF16),
        name="combine",
    )(returned[0], returned[1], *tables)


def add_levels(parts):
    levels, rows, width = parts.shape

    def kernel(p_ref, o_ref):
        total = p_ref[0].astype(F32)
        for level in range(1, levels):
            total = total + p_ref[level].astype(F32)
        o_ref[...] = total.astype(BF16)

    return pl.pallas_call(
        kernel,
        in_specs=[vspec()],
        out_specs=vspec(),
        out_shape=jax.ShapeDtypeStruct((rows, width), BF16),
        name="add_levels",
    )(parts)


def shifted(block, shift):
    copies = lax.axis_size("replica")
    return lax.ppermute(block, "replica", [(i, (i + shift) % copies) for i in range(copies)])


def level_groups():
    experts = lax.axis_size("expert")
    return [list(range(member, experts, PLANE)) for member in range(PLANE)]


def plane_groups():
    experts = lax.axis_size("expert")
    return [list(range(at, at + PLANE)) for at in range(0, experts, PLANE)]


def swapped(block):
    experts = lax.axis_size("expert")
    half = experts // 2
    return lax.ppermute(block, "expert", [(i, (i + half) % experts) for i in range(experts)])


def layer(
    hidden_first,
    hidden_second,
    routes_first,
    routes_second,
    mixing_first,
    mixing_second,
    norm_gain,
    expert_owner,
    swap_flags,
    gate_up_values,
    gate_up_scales,
    down_values,
    down_scales,
):
    experts = lax.axis_size("expert")
    copies = lax.axis_size("replica")
    my_slot = lax.axis_index("expert")
    my_copy = lax.axis_index("replica")
    features = hidden_first.shape[1]
    slot_ids = jnp.arange(experts, dtype=I32)

    current = (gate_up_values, gate_up_scales, down_values, down_scales)
    incoming = []
    for piece in current:
        incoming.append(swapped(piece))
    flagged = jnp.sum(jnp.where(slot_ids == my_slot, swap_flags, 0)) == 1

    expert_at = jnp.sum(
        jnp.where(expert_owner[:, None] == slot_ids[None, :], slot_ids[:, None], 0), axis=0
    )
    my_expert = jnp.sum(jnp.where(expert_owner == my_slot, slot_ids, 0)).reshape(1)
    hops = jnp.arange(copies, dtype=I32)
    ahead = (my_copy + hops) % copies
    behind = (my_copy - hops + copies) % copies

    ids = [
        jnp.pad(routes.astype(BF16), ((0, 0), (0, LANES - routes.shape[1])), constant_values=-1)
        for routes in (routes_first, routes_second)
    ]
    packs = norm_and_pack((hidden_first, hidden_second), ids, norm_gain.reshape(1, features))
    column = lax.all_gather(packs, "expert", axis=0, tiled=True, axis_index_groups=level_groups())
    gathered = lax.all_gather(
        column, "expert", axis=0, tiled=True, axis_index_groups=plane_groups()
    )

    gate_up_rows = jnp.repeat(gate_up_scales[0].astype(F32), LANES, axis=-1)
    down_rows = jnp.repeat(down_scales[0].astype(F32), LANES, axis=-1)
    down_sent = down_dequant(down_values[0], down_rows, ahead)
    down_weights = [down_sent[0]] + [shifted(down_sent[k], k) for k in range(1, copies)]
    gate_up_weights = gate_up_dequant(gate_up_values[0], gate_up_rows)
    picks = jnp.concatenate(
        [
            routes_first.astype(F32),
            mixing_first,
            routes_second.astype(F32),
            mixing_second,
        ],
        axis=1,
    )
    all_picks = lax.all_gather(picks, "replica", axis=0, tiled=True)
    all_picks = lax.all_gather(
        all_picks, "expert", axis=0, tiled=True, axis_index_groups=level_groups()
    )
    first = my_slot // PLANE * PLANE
    plane_experts = lax.dynamic_slice(expert_at, (first,), (PLANE,))
    plane_experts = jnp.repeat(plane_experts, copies * CAP).reshape(1, PLANE * copies * CAP)
    tables = mixing_tables(all_picks, plane_experts)

    chosen_rows = select_rows(gathered, my_expert)
    returned = []
    for step in range(2):
        own_rows = chosen_rows[step]
        pieces = [own_rows] + [shifted(own_rows, k) for k in range(1, copies)]
        inner = gate_up(pieces, gate_up_weights, behind)
        inners = [inner] + [shifted(inner, k) for k in range(1, copies)]
        results = down(inners, down_weights)
        back = lax.all_to_all(
            results.reshape(PLANE, experts // PLANE, copies * CAP, features // copies),
            "expert",
            split_axis=0,
            concat_axis=0,
            tiled=True,
            axis_index_groups=plane_groups(),
        )
        returned.append(back)

    mixed = combine(returned, tables, copies)
    levels = lax.all_to_all(
        mixed.reshape(experts // PLANE, copies * 2 * TOK, features // copies),
        "expert",
        split_axis=0,
        concat_axis=0,
        tiled=True,
        axis_index_groups=level_groups(),
    )
    summed = add_levels(levels).reshape(copies, 2 * TOK, features // copies)
    spread = lax.all_to_all(summed, "replica", split_axis=0, concat_axis=0, tiled=True)
    outputs = tuple(
        spread[:, step * TOK : (step + 1) * TOK].transpose(1, 0, 2).reshape(TOK, features)
        for step in range(2)
    )
    incoming = lax.optimization_barrier((*incoming, mixed))[: len(current)]
    moved = tuple(
        jnp.where(flagged, fresh, stale) for fresh, stale in zip(incoming, current)
    )
    return outputs + moved


def solution(mesh):
    tokens = P(("expert", "replica"), None)
    weights = (
        P("expert", None, None, "replica"),
        P("expert", None, None, "replica"),
        P("expert", "replica", None),
        P("expert", "replica", None),
    )
    return jax.shard_map(
        layer,
        mesh=mesh,
        in_specs=(tokens,) * 6 + (P(),) * 3 + weights,
        out_specs=(tokens,) * 2 + weights,
        check_vma=False,
    )
```

```python
import jax
import jax.numpy as jnp
from jax import lax
from jax.experimental import pallas as pl
from jax.experimental.pallas import tpu as pltpu
from jax.sharding import PartitionSpec as P


BF16 = jnp.bfloat16
F32 = jnp.float32
I32 = jnp.int32
TOK = 8
CAP = 2
LANES = 128
PLANE = 8
VMEM = pltpu.VMEM
SMEM = pltpu.SMEM


def iota(shape, dim):
    return lax.broadcasted_iota(I32, shape, dim)


def vspec():
    return pl.BlockSpec(memory_space=VMEM)


def sspec():
    return pl.BlockSpec(memory_space=SMEM)


def gate_up_dequant(values, scale_rows):
    _, features, width = values.shape
    rows = features // 4
    blocks = rows // LANES

    def kernel(v_ref, s_ref, o_ref):
        wide = v_ref[0].astype(F32).reshape(blocks, LANES, width)
        o_ref[0] = (wide * s_ref[0][:, None, :]).reshape(rows, width).astype(BF16)

    return pl.pallas_call(
        kernel,
        grid=(2, 4),
        in_specs=[
            pl.BlockSpec((1, rows, width), lambda g, i: (g, i, 0)),
            pl.BlockSpec((1, blocks, width), lambda g, i: (g, i, 0)),
        ],
        out_specs=pl.BlockSpec((1, rows, width), lambda g, i: (g, i, 0)),
        out_shape=jax.ShapeDtypeStruct(values.shape, BF16),
        name="gate_up_dequant",
    )(values, scale_rows)


def down_dequant(values, scale_rows, order):
    height, features = values.shape
    copies = order.shape[0]
    width = features // copies
    blocks = scale_rows.shape[0]

    def kernel(order_ref, v_ref, s_ref, o_ref):
        wide = v_ref[...].astype(F32).reshape(blocks, height // blocks, width)
        o_ref[0] = (wide * s_ref[...][:, None, :]).reshape(height, width).astype(BF16)

    return pl.pallas_call(
        kernel,
        grid_spec=pltpu.PrefetchScalarGridSpec(
            num_scalar_prefetch=1,
            grid=(copies,),
            in_specs=[
                pl.BlockSpec((height, width), lambda k, o: (0, o[k])),
                pl.BlockSpec((blocks, width), lambda k, o: (0, o[k])),
            ],
            out_specs=pl.BlockSpec((1, height, width), lambda k, o: (k, 0, 0)),
        ),
        out_shape=jax.ShapeDtypeStruct((copies, height, width), BF16),
        name="down_dequant",
    )(order, values, scale_rows)


def norm_and_pack(hidden, routes, mixing, gain, levels):
    rows, features = hidden[0].shape
    top = routes[0].shape[1]

    def kernel(h0, h1, r0, r1, m0, m1, g_ref, o_ref):
        lane, entry = iota((top, LANES), 1), iota((top, LANES), 0)
        for at, h_ref, r_ref, m_ref in ((0, h0, r0, m0), (rows, h1, r1, m1)):
            wide = h_ref[...].astype(F32)
            inverse = lax.rsqrt(jnp.mean(wide * wide, axis=-1, keepdims=True) + 1e-06)
            normed = (wide * inverse * g_ref[...]).astype(BF16)
            high = m_ref[...].astype(BF16)
            rest = m_ref[...] - high.astype(F32)
            middle = rest.astype(BF16)
            low = (rest - middle.astype(F32)).astype(BF16)
            picks = jnp.zeros((rows, LANES), F32)
            for part, values in enumerate((r_ref[...].astype(F32).astype(BF16), high, middle, low)):
                put = jnp.where(lane == entry + part * top, 1.0, 0.0).astype(BF16)
                picks = picks + jnp.dot(values, put, preferred_element_type=F32)
            picks = picks.astype(BF16)
            for level in range(levels):
                o_ref[level, at : at + rows, :features] = normed
                o_ref[level, at : at + rows, features:] = picks

    return pl.pallas_call(
        kernel,
        in_specs=[vspec()] * 7,
        out_specs=vspec(),
        out_shape=jax.ShapeDtypeStruct((levels, 2 * rows, features + LANES), BF16),
        name="norm_and_pack",
    )(*hidden, *routes, *mixing, gain)


def select_rows(column, plane_experts, top):
    rows, packed = column.shape
    features = packed - LANES
    groups = rows // TOK
    kept = PLANE * groups * CAP

    def kernel(e_ref, c_ref, o_ref):
        at = e_ref[...].astype(F32)
        ids = c_ref[:, features:].astype(F32)
        hit = jnp.zeros((rows, kept), F32)
        for k in range(top):
            hit = hit + jnp.where(ids[:, k : k + 1] == at, 1.0, 0.0)
        r, q = iota((rows, rows), 0), iota((rows, rows), 1)
        before = jnp.where(((r >> 3) == (q >> 3)) & (q < r), 1.0, 0.0).astype(BF16)
        rank = jnp.dot(before, hit.astype(BF16), preferred_element_type=F32)
        row, col = iota((rows, kept), 0), iota((rows, kept), 1)
        own_group = (row >> 3) == ((col >> 1) & (groups - 1))
        chosen = own_group & (rank == (col & 1).astype(F32)) & (hit > 0.5)
        picking = jnp.where(chosen, 1.0, 0.0).astype(BF16)
        for start in range(0, features, 1024):
            o_ref[:, start : start + 1024] = lax.dot_general(
                picking,
                c_ref[:, start : start + 1024],
                (((0,), (0,)), ((), ())),
                preferred_element_type=F32,
            ).astype(BF16)

    return pl.pallas_call(
        kernel,
        in_specs=[vspec(), vspec()],
        out_specs=vspec(),
        out_shape=jax.ShapeDtypeStruct((kept, features), BF16),
        name="select_rows",
    )(jnp.repeat(plane_experts, groups * CAP).reshape(1, kept), column)


def gate_up(pieces, weights, columns):
    copies = len(pieces)
    rows, features = pieces[0].shape
    width = weights.shape[2]

    def kernel(c_ref, *refs):
        x_refs, w_ref, o_ref, x_all = refs[:copies], refs[copies], refs[copies + 1], refs[copies + 2]
        for k in range(copies):
            start = pl.multiple_of(c_ref[k] * rows, rows)
            x_all[pl.ds(start, rows), :] = x_refs[k][...]
        gate = jnp.dot(x_all[...], w_ref[0], preferred_element_type=F32)
        up = jnp.dot(x_all[...], w_ref[1], preferred_element_type=F32)
        o_ref[...] = (gate / (1.0 + jnp.exp(-gate)) * up).astype(BF16)

    return pl.pallas_call(
        kernel,
        in_specs=[sspec()] + [vspec()] * (copies + 1),
        out_specs=vspec(),
        out_shape=jax.ShapeDtypeStruct((copies * rows, width), BF16),
        scratch_shapes=[pltpu.VMEM((copies * rows, features), BF16)],
        name="gate_up",
    )(columns, *pieces, weights)


def down(inner, weights):
    copies = len(inner)
    rows, width_in = inner[0].shape
    width = weights[0].shape[1]
    piece = rows // copies // PLANE
    group = piece * copies
    unit = 2 * CAP

    def kernel(*refs):
        i_refs, w_refs, o_ref, placed = (
            refs[:copies],
            refs[copies : 2 * copies],
            refs[2 * copies],
            refs[2 * copies + 1],
        )
        r, q = iota((group, group), 0), iota((group, group), 1)
        copy, level = (r >> 2) & (copies - 1), r >> 4
        source = copy * piece + level * unit + (r & 3)
        order = jnp.where(q == source, 1.0, 0.0).astype(BF16)
        total = jnp.zeros((rows, width), F32)
        for i_ref, w_ref in zip(i_refs, w_refs):
            for member in range(PLANE):
                parts = [
                    i_ref[(c * PLANE + member) * piece : (c * PLANE + member + 1) * piece, :]
                    for c in range(copies)
                ]
                placed[member * group : (member + 1) * group, :] = jnp.dot(
                    order, jnp.concatenate(parts, axis=0), preferred_element_type=F32
                ).astype(BF16)
            total = total + jnp.dot(placed[...], w_ref[...], preferred_element_type=F32)
        o_ref[...] = total.astype(BF16)

    return pl.pallas_call(
        kernel,
        in_specs=[vspec()] * (2 * copies),
        out_specs=vspec(),
        out_shape=jax.ShapeDtypeStruct((rows, width), BF16),
        scratch_shapes=[pltpu.VMEM((rows, width_in), BF16)],
        name="down",
    )(*inner, *weights)


def mixing_tables(picks, plane_experts, copies, top):
    tokens = picks.shape[0]
    places = PLANE * copies * 2 * CAP
    column = tokens // copies

    def kernel(p_ref, e_ref, high_ref, low_ref):
        at = e_ref[...].astype(F32)
        packed = p_ref[...].astype(F32)
        hit = jnp.zeros((tokens, places), F32)
        weight = jnp.zeros((tokens, places), F32)
        for k in range(top):
            same = packed[:, k : k + 1] == at
            mix = (
                packed[:, top + k : top + k + 1]
                + packed[:, 2 * top + k : 2 * top + k + 1]
                + packed[:, 3 * top + k : 3 * top + k + 1]
            )
            hit = hit + jnp.where(same, 1.0, 0.0)
            weight = weight + jnp.where(same, mix, 0.0)
        r, q = iota((column, column), 0), iota((column, column), 1)
        before = jnp.where(((r >> 3) == (q >> 3)) & (q < r), 1.0, 0.0).astype(BF16)
        row, col = iota((column, places), 0), iota((column, places), 1)
        for copy in range(copies):
            rows = slice(copy * column, (copy + 1) * column)
            rank = jnp.dot(before, hit[rows].astype(BF16), preferred_element_type=F32)
            here = (
                (((col >> 2) & (copies - 1)) == copy)
                & (((row >> 3) & 1) == ((col >> 1) & 1))
                & (rank == (col & 1).astype(F32))
            )
            kept = jnp.where(here, weight[rows], 0.0)
            high = kept.astype(BF16)
            high_ref[rows, :] = high
            low_ref[rows, :] = (kept - high.astype(F32)).astype(BF16)

    shape = jax.ShapeDtypeStruct((tokens, places), BF16)
    return pl.pallas_call(
        kernel,
        in_specs=[vspec(), vspec()],
        out_specs=[vspec()] * 2,
        out_shape=[shape] * 2,
        name="mixing_tables",
    )(picks, jnp.repeat(plane_experts, copies * 2 * CAP).reshape(1, places))


def combine(returned, tables, copies):
    members, levels, rows, width = returned.shape
    tokens = copies * 2 * TOK
    column = levels * 2 * TOK

    def kernel(r_ref, h_ref, l_ref, o_ref):
        for level in range(levels):
            found = r_ref[:, level].reshape(members * rows, width)
            total = jnp.zeros((tokens, width), F32)
            for t_ref in (h_ref, l_ref):
                first = level * 2 * TOK
                table = jnp.concatenate(
                    [
                        t_ref[c * column + first : c * column + first + 2 * TOK, :]
                        for c in range(copies)
                    ],
                    axis=0,
                )
                total = total + jnp.dot(table, found, preferred_element_type=F32)
            o_ref[level] = total.astype(BF16)

    return pl.pallas_call(
        kernel,
        in_specs=[vspec()] * 3,
        out_specs=vspec(),
        out_shape=jax.ShapeDtypeStruct((levels, tokens, width), BF16),
        name="combine",
    )(returned, *tables)


def add_levels(parts):
    levels, rows, width = parts.shape

    def kernel(p_ref, o_ref):
        total = p_ref[0].astype(F32)
        for level in range(1, levels):
            total = total + p_ref[level].astype(F32)
        o_ref[...] = total.astype(BF16)

    return pl.pallas_call(
        kernel,
        in_specs=[vspec()],
        out_specs=vspec(),
        out_shape=jax.ShapeDtypeStruct((rows, width), BF16),
        name="add_levels",
    )(parts)


def shifted(block, shift):
    copies = lax.axis_size("replica")
    return lax.ppermute(block, "replica", [(i, (i + shift) % copies) for i in range(copies)])


def level_groups():
    experts = lax.axis_size("expert")
    return [list(range(member, experts, PLANE)) for member in range(PLANE)]


def plane_groups():
    experts = lax.axis_size("expert")
    return [list(range(at, at + PLANE)) for at in range(0, experts, PLANE)]


def swapped(block):
    experts = lax.axis_size("expert")
    half = experts // 2
    return lax.ppermute(block, "expert", [(i, (i + half) % experts) for i in range(experts)])


def layer(
    hidden_first,
    hidden_second,
    routes_first,
    routes_second,
    mixing_first,
    mixing_second,
    norm_gain,
    expert_owner,
    swap_flags,
    gate_up_values,
    gate_up_scales,
    down_values,
    down_scales,
):
    experts = lax.axis_size("expert")
    copies = lax.axis_size("replica")
    levels = experts // PLANE
    my_slot = lax.axis_index("expert")
    my_copy = lax.axis_index("replica")
    features = hidden_first.shape[1]
    width = features // copies
    top = routes_first.shape[1]
    slot_ids = jnp.arange(experts, dtype=I32)
    hops = jnp.arange(copies, dtype=I32)
    ahead = (my_copy + hops) % copies
    behind = (my_copy - hops + copies) % copies

    plane_slots = my_slot // PLANE * PLANE + jnp.arange(PLANE, dtype=I32)
    plane_experts = jnp.sum(
        jnp.where(expert_owner[:, None] == plane_slots[None, :], slot_ids[:, None], 0), axis=0
    )

    packs = norm_and_pack(
        (hidden_first, hidden_second),
        (routes_first, routes_second),
        (mixing_first, mixing_second),
        norm_gain.reshape(1, features),
        levels,
    )
    column = lax.all_to_all(
        packs, "expert", 0, 0, tiled=True, axis_index_groups=level_groups()
    )
    column = column.reshape(levels * 2 * TOK, features + LANES)

    flagged = jnp.sum(jnp.where(slot_ids == my_slot, swap_flags, 0)) == 1
    cut = down_values.shape[1] * 13 // 16
    early_piece, late_piece = down_values[0, :cut], down_values[0, cut:]
    gate_up_in = swapped(gate_up_values)
    scales = (gate_up_scales, down_scales)
    tail = jnp.concatenate([scale.reshape(-1) for scale in scales])
    tail = jnp.pad(tail, (0, TOK * features - tail.size)).reshape(TOK, features)
    early_in = swapped(jnp.concatenate([early_piece, tail]))

    own_rows = select_rows(column, plane_experts, top)
    own_rows = lax.all_to_all(
        own_rows.reshape(PLANE, -1, features),
        "expert",
        0,
        0,
        tiled=True,
        axis_index_groups=plane_groups(),
    ).reshape(own_rows.shape)

    picks = lax.all_gather(column[:, features:], "replica", axis=0, tiled=True)
    tables = mixing_tables(picks, plane_experts, copies, top)
    gate_up_rows = jnp.repeat(gate_up_scales[0].astype(F32), LANES, axis=-1)
    down_rows = jnp.repeat(down_scales[0].astype(F32), LANES, axis=-1)
    down_sent = down_dequant(down_values[0], down_rows, ahead)
    down_weights = [down_sent[0]] + [shifted(down_sent[k], k) for k in range(1, copies)]
    gate_up_weights = gate_up_dequant(gate_up_values[0], gate_up_rows)

    pieces = [own_rows] + [shifted(own_rows, k) for k in range(1, copies)]

    inner = gate_up(pieces, gate_up_weights, behind)
    inners = [inner] + [shifted(inner, k) for k in range(1, copies)]
    results = down(inners, down_weights)
    returned = lax.all_to_all(
        results.reshape(PLANE, levels, -1, width),
        "expert",
        0,
        0,
        tiled=True,
        axis_index_groups=plane_groups(),
    )
    mixed = combine(returned, tables, copies)
    parts = lax.all_to_all(
        mixed, "expert", 0, 0, tiled=True, axis_index_groups=level_groups()
    )
    late_in = swapped(late_piece)
    summed = add_levels(parts).reshape(copies, 2 * TOK, width)
    spread = lax.all_to_all(summed, "replica", split_axis=0, concat_axis=0, tiled=True)
    outputs = tuple(
        spread[:, step * TOK : (step + 1) * TOK].transpose(1, 0, 2).reshape(TOK, features)
        for step in range(2)
    )

    gate_up_in, early_in, _ = lax.optimization_barrier((gate_up_in, early_in, mixed))
    tail_in = early_in[cut]
    count = gate_up_scales.size
    scales_in = (
        tail_in[:count].reshape(gate_up_scales.shape),
        tail_in[count : count + down_scales.size].reshape(down_scales.shape),
    )
    gate_up_moved = jnp.where(flagged, gate_up_in, gate_up_values)
    gate_up_scales_moved = jnp.where(flagged, scales_in[0], gate_up_scales)
    down_scales_moved = jnp.where(flagged, scales_in[1], down_scales)
    down_in = jnp.concatenate([early_in[:cut], late_in])[None]
    down_moved = jnp.where(flagged, down_in, down_values)
    return outputs + (gate_up_moved, gate_up_scales_moved, down_moved, down_scales_moved)


def solution(mesh):
    tokens = P(("expert", "replica"), None)
    weights = (
        P("expert", None, None, "replica"),
        P("expert", None, None, "replica"),
        P("expert", "replica", None),
        P("expert", "replica", None),
    )
    return jax.shard_map(
        layer,
        mesh=mesh,
        in_specs=(tokens,) * 6 + (P(),) * 3 + weights,
        out_specs=(tokens,) * 2 + weights,
        check_vma=False,
    )
```

```python
import jax
import jax.numpy as jnp
from jax import lax
from jax.experimental import pallas as pl
from jax.experimental.pallas import tpu as pltpu
from jax.sharding import PartitionSpec as P


BF16 = jnp.bfloat16
F32 = jnp.float32
I32 = jnp.int32
TOK = 8
CAP = 2
LANES = 128
PLANE = 8
VMEM = pltpu.VMEM
SMEM = pltpu.SMEM


def iota(shape, dim):
    return lax.broadcasted_iota(I32, shape, dim)


def vspec():
    return pl.BlockSpec(memory_space=VMEM)


def sspec():
    return pl.BlockSpec(memory_space=SMEM)


def gate_up_dequant(values, scale_rows):
    _, features, width = values.shape
    rows = features // 4
    blocks = rows // LANES

    def kernel(v_ref, s_ref, o_ref):
        wide = v_ref[0].astype(F32).reshape(blocks, LANES, width)
        o_ref[0] = (wide * s_ref[0][:, None, :]).reshape(rows, width).astype(BF16)

    return pl.pallas_call(
        kernel,
        grid=(2, 4),
        in_specs=[
            pl.BlockSpec((1, rows, width), lambda g, i: (g, i, 0)),
            pl.BlockSpec((1, blocks, width), lambda g, i: (g, i, 0)),
        ],
        out_specs=pl.BlockSpec((1, rows, width), lambda g, i: (g, i, 0)),
        out_shape=jax.ShapeDtypeStruct(values.shape, BF16),
        name="gate_up_dequant",
    )(values, scale_rows)


def down_dequant(values, scale_rows, order):
    height, features = values.shape
    copies = order.shape[0]
    width = features // copies
    blocks = scale_rows.shape[0]

    def kernel(order_ref, v_ref, s_ref, o_ref):
        wide = v_ref[...].astype(F32).reshape(blocks, height // blocks, width)
        o_ref[0] = (wide * s_ref[...][:, None, :]).reshape(height, width).astype(BF16)

    return pl.pallas_call(
        kernel,
        grid_spec=pltpu.PrefetchScalarGridSpec(
            num_scalar_prefetch=1,
            grid=(copies,),
            in_specs=[
                pl.BlockSpec((height, width), lambda k, o: (0, o[k])),
                pl.BlockSpec((blocks, width), lambda k, o: (0, o[k])),
            ],
            out_specs=pl.BlockSpec((1, height, width), lambda k, o: (k, 0, 0)),
        ),
        out_shape=jax.ShapeDtypeStruct((copies, height, width), BF16),
        name="down_dequant",
    )(order, values, scale_rows)


def norm_and_pack(hidden, routes, mixing, gain, levels):
    rows, features = hidden[0].shape
    top = routes[0].shape[1]

    def kernel(h0, h1, r0, r1, m0, m1, g_ref, o_ref):
        lane, entry = iota((top, LANES), 1), iota((top, LANES), 0)
        for at, h_ref, r_ref, m_ref in ((0, h0, r0, m0), (rows, h1, r1, m1)):
            wide = h_ref[...].astype(F32)
            inverse = lax.rsqrt(jnp.mean(wide * wide, axis=-1, keepdims=True) + 1e-06)
            normed = (wide * inverse * g_ref[...]).astype(BF16)
            high = m_ref[...].astype(BF16)
            rest = m_ref[...] - high.astype(F32)
            middle = rest.astype(BF16)
            low = (rest - middle.astype(F32)).astype(BF16)
            picks = jnp.zeros((rows, LANES), F32)
            for part, values in enumerate((r_ref[...].astype(F32).astype(BF16), high, middle, low)):
                put = jnp.where(lane == entry + part * top, 1.0, 0.0).astype(BF16)
                picks = picks + jnp.dot(values, put, preferred_element_type=F32)
            picks = picks.astype(BF16)
            for level in range(levels):
                o_ref[level, at : at + rows, :features] = normed
                o_ref[level, at : at + rows, features:] = picks

    return pl.pallas_call(
        kernel,
        in_specs=[vspec()] * 7,
        out_specs=vspec(),
        out_shape=jax.ShapeDtypeStruct((levels, 2 * rows, features + LANES), BF16),
        name="norm_and_pack",
    )(*hidden, *routes, *mixing, gain)


def select_rows(column, plane_experts, top):
    rows, packed = column.shape
    features = packed - LANES
    groups = rows // TOK
    kept = PLANE * groups * CAP

    def kernel(e_ref, c_ref, o_ref):
        at = e_ref[...].astype(F32)
        ids = c_ref[:, features:].astype(F32)
        hit = jnp.zeros((rows, kept), F32)
        for k in range(top):
            hit = hit + jnp.where(ids[:, k : k + 1] == at, 1.0, 0.0)
        r, q = iota((rows, rows), 0), iota((rows, rows), 1)
        before = jnp.where(((r >> 3) == (q >> 3)) & (q < r), 1.0, 0.0).astype(BF16)
        rank = jnp.dot(before, hit.astype(BF16), preferred_element_type=F32)
        row, col = iota((rows, kept), 0), iota((rows, kept), 1)
        own_group = (row >> 3) == ((col >> 1) & (groups - 1))
        chosen = own_group & (rank == (col & 1).astype(F32)) & (hit > 0.5)
        picking = jnp.where(chosen, 1.0, 0.0).astype(BF16)
        for start in range(0, features, 1024):
            o_ref[:, start : start + 1024] = lax.dot_general(
                picking,
                c_ref[:, start : start + 1024],
                (((0,), (0,)), ((), ())),
                preferred_element_type=F32,
            ).astype(BF16)

    return pl.pallas_call(
        kernel,
        in_specs=[vspec(), vspec()],
        out_specs=vspec(),
        out_shape=jax.ShapeDtypeStruct((kept, features), BF16),
        name="select_rows",
    )(jnp.repeat(plane_experts, groups * CAP).reshape(1, kept), column)


def gate_up(pieces, weights, columns):
    copies = len(pieces)
    rows, features = pieces[0].shape
    width = weights.shape[2]

    def kernel(c_ref, *refs):
        x_refs, w_ref, o_ref, x_all = refs[:copies], refs[copies], refs[copies + 1], refs[copies + 2]
        for k in range(copies):
            start = pl.multiple_of(c_ref[k] * rows, rows)
            x_all[pl.ds(start, rows), :] = x_refs[k][...]
        gate = jnp.dot(x_all[...], w_ref[0], preferred_element_type=F32)
        up = jnp.dot(x_all[...], w_ref[1], preferred_element_type=F32)
        o_ref[...] = (gate / (1.0 + jnp.exp(-gate)) * up).astype(BF16)

    return pl.pallas_call(
        kernel,
        in_specs=[sspec()] + [vspec()] * (copies + 1),
        out_specs=vspec(),
        out_shape=jax.ShapeDtypeStruct((copies * rows, width), BF16),
        scratch_shapes=[pltpu.VMEM((copies * rows, features), BF16)],
        name="gate_up",
    )(columns, *pieces, weights)


def down(inner, weights):
    copies = len(inner)
    rows, width_in = inner[0].shape
    width = weights[0].shape[1]
    piece = rows // copies // PLANE
    group = piece * copies
    unit = 2 * CAP

    def kernel(*refs):
        i_refs, w_refs, o_ref, placed = (
            refs[:copies],
            refs[copies : 2 * copies],
            refs[2 * copies],
            refs[2 * copies + 1],
        )
        r, q = iota((group, group), 0), iota((group, group), 1)
        copy, level = (r >> 2) & (copies - 1), r >> 4
        source = copy * piece + level * unit + (r & 3)
        order = jnp.where(q == source, 1.0, 0.0).astype(BF16)
        total = jnp.zeros((rows, width), F32)
        for i_ref, w_ref in zip(i_refs, w_refs):
            for member in range(PLANE):
                parts = [
                    i_ref[(c * PLANE + member) * piece : (c * PLANE + member + 1) * piece, :]
                    for c in range(copies)
                ]
                placed[member * group : (member + 1) * group, :] = jnp.dot(
                    order, jnp.concatenate(parts, axis=0), preferred_element_type=F32
                ).astype(BF16)
            total = total + jnp.dot(placed[...], w_ref[...], preferred_element_type=F32)
        o_ref[...] = total.astype(BF16)

    return pl.pallas_call(
        kernel,
        in_specs=[vspec()] * (2 * copies),
        out_specs=vspec(),
        out_shape=jax.ShapeDtypeStruct((rows, width), BF16),
        scratch_shapes=[pltpu.VMEM((rows, width_in), BF16)],
        name="down",
    )(*inner, *weights)


def mixing_tables(picks, plane_experts, copies, top):
    tokens = picks.shape[0]
    places = PLANE * copies * 2 * CAP
    column = tokens // copies

    def kernel(p_ref, e_ref, high_ref, low_ref):
        at = e_ref[...].astype(F32)
        packed = p_ref[...].astype(F32)
        hit = jnp.zeros((tokens, places), F32)
        weight = jnp.zeros((tokens, places), F32)
        for k in range(top):
            same = packed[:, k : k + 1] == at
            mix = (
                packed[:, top + k : top + k + 1]
                + packed[:, 2 * top + k : 2 * top + k + 1]
                + packed[:, 3 * top + k : 3 * top + k + 1]
            )
            hit = hit + jnp.where(same, 1.0, 0.0)
            weight = weight + jnp.where(same, mix, 0.0)
        r, q = iota((column, column), 0), iota((column, column), 1)
        before = jnp.where(((r >> 3) == (q >> 3)) & (q < r), 1.0, 0.0).astype(BF16)
        row, col = iota((column, places), 0), iota((column, places), 1)
        for copy in range(copies):
            rows = slice(copy * column, (copy + 1) * column)
            rank = jnp.dot(before, hit[rows].astype(BF16), preferred_element_type=F32)
            here = (
                (((col >> 2) & (copies - 1)) == copy)
                & (((row >> 3) & 1) == ((col >> 1) & 1))
                & (rank == (col & 1).astype(F32))
            )
            kept = jnp.where(here, weight[rows], 0.0)
            high = kept.astype(BF16)
            high_ref[rows, :] = high
            low_ref[rows, :] = (kept - high.astype(F32)).astype(BF16)

    shape = jax.ShapeDtypeStruct((tokens, places), BF16)
    return pl.pallas_call(
        kernel,
        in_specs=[vspec(), vspec()],
        out_specs=[vspec()] * 2,
        out_shape=[shape] * 2,
        name="mixing_tables",
    )(picks, jnp.repeat(plane_experts, copies * 2 * CAP).reshape(1, places))


def combine(returned, tables, copies):
    members, levels, rows, width = returned.shape
    tokens = copies * 2 * TOK
    column = levels * 2 * TOK

    def kernel(r_ref, h_ref, l_ref, o_ref):
        for level in range(levels):
            found = r_ref[:, level].reshape(members * rows, width)
            total = jnp.zeros((tokens, width), F32)
            for t_ref in (h_ref, l_ref):
                first = level * 2 * TOK
                table = jnp.concatenate(
                    [
                        t_ref[c * column + first : c * column + first + 2 * TOK, :]
                        for c in range(copies)
                    ],
                    axis=0,
                )
                total = total + jnp.dot(table, found, preferred_element_type=F32)
            o_ref[level] = total.astype(BF16)

    return pl.pallas_call(
        kernel,
        in_specs=[vspec()] * 3,
        out_specs=vspec(),
        out_shape=jax.ShapeDtypeStruct((levels, tokens, width), BF16),
        name="combine",
    )(returned, *tables)


def add_levels(parts):
    levels, rows, width = parts.shape

    def kernel(p_ref, o_ref):
        total = p_ref[0].astype(F32)
        for level in range(1, levels):
            total = total + p_ref[level].astype(F32)
        o_ref[...] = total.astype(BF16)

    return pl.pallas_call(
        kernel,
        in_specs=[vspec()],
        out_specs=vspec(),
        out_shape=jax.ShapeDtypeStruct((rows, width), BF16),
        name="add_levels",
    )(parts)


def place_rows(flag, fresh, stale, first, count, filled=None):
    unit = 2 * TOK
    height, features = stale.shape
    start = first // unit

    def kernel(f_ref, n_ref, s_ref, *refs):
        refs[-1][...] = jnp.where(f_ref[0] == 1, n_ref[...], s_ref[...])

    in_specs = [
        sspec(),
        pl.BlockSpec((unit, features), lambda i: (i, 0)),
        pl.BlockSpec((unit, features), lambda i: (start + i, 0)),
    ]
    given = [flag, fresh, stale]
    if filled is not None:
        in_specs.append(pl.BlockSpec(memory_space=pl.ANY))
        given.append(filled)
    return pl.pallas_call(
        kernel,
        grid=(count // unit,),
        in_specs=in_specs,
        out_specs=pl.BlockSpec((unit, features), lambda i: (start + i, 0)),
        out_shape=jax.ShapeDtypeStruct((height, features), BF16),
        input_output_aliases={} if filled is None else {3: 0},
        name="early_rows" if filled is None else "late_rows",
    )(*given)


def shifted(block, shift):
    copies = lax.axis_size("replica")
    return lax.ppermute(block, "replica", [(i, (i + shift) % copies) for i in range(copies)])


def level_groups():
    experts = lax.axis_size("expert")
    return [list(range(member, experts, PLANE)) for member in range(PLANE)]


def plane_groups():
    experts = lax.axis_size("expert")
    return [list(range(at, at + PLANE)) for at in range(0, experts, PLANE)]


def swapped(block):
    experts = lax.axis_size("expert")
    half = experts // 2
    return lax.ppermute(block, "expert", [(i, (i + half) % experts) for i in range(experts)])


def layer(
    hidden_first,
    hidden_second,
    routes_first,
    routes_second,
    mixing_first,
    mixing_second,
    norm_gain,
    expert_owner,
    swap_flags,
    gate_up_values,
    gate_up_scales,
    down_values,
    down_scales,
):
    experts = lax.axis_size("expert")
    copies = lax.axis_size("replica")
    levels = experts // PLANE
    my_slot = lax.axis_index("expert")
    my_copy = lax.axis_index("replica")
    features = hidden_first.shape[1]
    width = features // copies
    top = routes_first.shape[1]
    slot_ids = jnp.arange(experts, dtype=I32)
    hops = jnp.arange(copies, dtype=I32)
    ahead = (my_copy + hops) % copies
    behind = (my_copy - hops + copies) % copies

    plane_slots = my_slot // PLANE * PLANE + jnp.arange(PLANE, dtype=I32)
    plane_experts = jnp.sum(
        jnp.where(expert_owner[:, None] == plane_slots[None, :], slot_ids[:, None], 0), axis=0
    )

    packs = norm_and_pack(
        (hidden_first, hidden_second),
        (routes_first, routes_second),
        (mixing_first, mixing_second),
        norm_gain.reshape(1, features),
        levels,
    )
    column = lax.all_to_all(
        packs, "expert", 0, 0, tiled=True, axis_index_groups=level_groups()
    )
    column = column.reshape(levels * 2 * TOK, features + LANES)

    flagged = jnp.sum(jnp.where(slot_ids == my_slot, swap_flags, 0)) == 1
    cut = down_values.shape[1] * 13 // 16
    early_piece, late_piece = down_values[0, :cut], down_values[0, cut:]
    gate_up_in = swapped(gate_up_values)
    scales = (gate_up_scales, down_scales)
    tail = jnp.concatenate([scale.reshape(-1) for scale in scales])
    tail = jnp.pad(tail, (0, TOK * features - tail.size)).reshape(TOK, features)
    early_in = swapped(jnp.concatenate([early_piece, tail]))

    own_rows = select_rows(column, plane_experts, top)
    own_rows = lax.all_to_all(
        own_rows.reshape(PLANE, -1, features),
        "expert",
        0,
        0,
        tiled=True,
        axis_index_groups=plane_groups(),
    ).reshape(own_rows.shape)

    picks = lax.all_gather(column[:, features:], "replica", axis=0, tiled=True)
    tables = mixing_tables(picks, plane_experts, copies, top)
    gate_up_rows = jnp.repeat(gate_up_scales[0].astype(F32), LANES, axis=-1)
    down_rows = jnp.repeat(down_scales[0].astype(F32), LANES, axis=-1)
    down_sent = down_dequant(down_values[0], down_rows, ahead)
    down_weights = [down_sent[0]] + [shifted(down_sent[k], k) for k in range(1, copies)]
    gate_up_weights = gate_up_dequant(gate_up_values[0], gate_up_rows)

    pieces = [own_rows] + [shifted(own_rows, k) for k in range(1, copies)]

    inner = gate_up(pieces, gate_up_weights, behind)
    inners = [inner] + [shifted(inner, k) for k in range(1, copies)]
    results = down(inners, down_weights)
    returned = lax.all_to_all(
        results.reshape(PLANE, levels, -1, width),
        "expert",
        0,
        0,
        tiled=True,
        axis_index_groups=plane_groups(),
    )
    mixed = combine(returned, tables, copies)
    parts = lax.all_to_all(
        mixed, "expert", 0, 0, tiled=True, axis_index_groups=level_groups()
    )
    late_in = swapped(late_piece)
    summed = add_levels(parts).reshape(copies, 2 * TOK, width)
    spread = lax.all_to_all(summed, "replica", split_axis=0, concat_axis=0, tiled=True)
    outputs = tuple(
        spread[:, step * TOK : (step + 1) * TOK].transpose(1, 0, 2).reshape(TOK, features)
        for step in range(2)
    )

    gate_up_in, early_in, _ = lax.optimization_barrier((gate_up_in, early_in, mixed))
    tail_in = early_in[cut]
    count = gate_up_scales.size
    scales_in = (
        tail_in[:count].reshape(gate_up_scales.shape),
        tail_in[count : count + down_scales.size].reshape(down_scales.shape),
    )
    gate_up_moved = jnp.where(flagged, gate_up_in, gate_up_values)
    gate_up_scales_moved = jnp.where(flagged, scales_in[0], gate_up_scales)
    down_scales_moved = jnp.where(flagged, scales_in[1], down_scales)
    flag = flagged.astype(I32).reshape(1)
    down_moved = place_rows(flag, early_in, down_values[0], 0, cut)
    late_rows = down_values.shape[1] - cut
    down_moved = place_rows(flag, late_in, down_values[0], cut, late_rows, down_moved)[None]
    return outputs + (gate_up_moved, gate_up_scales_moved, down_moved, down_scales_moved)


def solution(mesh):
    tokens = P(("expert", "replica"), None)
    weights = (
        P("expert", None, None, "replica"),
        P("expert", None, None, "replica"),
        P("expert", "replica", None),
        P("expert", "replica", None),
    )
    return jax.shard_map(
        layer,
        mesh=mesh,
        in_specs=(tokens,) * 6 + (P(),) * 3 + weights,
        out_specs=(tokens,) * 2 + weights,
        check_vma=False,
    )
```
